32 devices in a mesh: grp: 2 (over y), lon: 16 (over z, x, core).
Axes of the slice: x: 2, y: 2, z: 4, core: 2. Of those that a mesh axis runs over, the one named last changes fastest.
Arguments:
- base_state: bfloat16 [384, 6, 768], P(('grp', 'lon')), parts along dimension 0, may hold values from -6 to 6
- tangents: bfloat16 [2, 384, 6, 768], P(None, ('grp', 'lon')), parts along dimension 1, may hold values from -120 to 120
- norm_gain: float32 [192], replicated, may hold values from 0.25 to 1.75
- qkv_weight: bfloat16 [192, 576], replicated, may hold values from -0.4375 to 0.4375
- out_weight: bfloat16 [192, 192], replicated, may hold values from -0.4375 to 0.4375
- bias_table: float32 [2, 3312, 6], replicated, may hold values from -2 to 306
- bias_index: int32 [144, 144], replicated, may hold values from 0 to 3311
- region: int32 [6, 4], replicated, may hold values from 0 to 2
- energy_table: float32 [3, 192], replicated, may hold values from 0.3 to 3
- level_class: int32 [4], replicated, may hold values from 0 to 2
Outputs:
- singular: float32 [2, 384, 6, 768], P(None, ('grp', 'lon')), parts along dimension 1
The draws below stay inside these ranges and needn't reach their ends.
There are 2 independent parts, one for each index of `grp`. The reference program is written for one: setup_inputs(seed, part) draws one part's arguments, and reference() takes and returns one part's arrays. A program takes and returns all parts, laid end to end along the dimension named above; an argument that names none is the same for every part. Nothing has to cross between parts.
All inputs are finite; a program needn't handle non-finite values.
Results may differ from the reference program's by a relative error of at most 0.015.
Values may be sent and summed in bfloat16 or wider, within the bound.
No kernel may reach another device: no remote copies, remote signals or barrier semaphores. Data moves between devices by JAX's collectives and lax.ppermute only.
A program may use at most 128 MiB of HBM per device.

```python
import math
import jax
import jax.numpy as jnp
from jax import lax

C = 192
HEADS = 6
HEAD = 32
WLON = 12
WLAT = 6
WLEV = 2
LEV = 4
ECLS = 3
LAT = 6
LON = 192
WTYPES = 2
NPOS = 3312


def draw_tangents(key, part):
    noise_key, lat_key, chan_key = jax.random.split(key, 3)
    shape = (2, LON, LAT, LEV * C)
    ramp = jnp.exp(jnp.log(3.0) * jnp.arange(LON, dtype=jnp.float32) / LON).reshape(1, LON, 1, 1)
    lat_scale = 10.0 ** jax.random.uniform(lat_key, (1, 1, LAT, 1), minval=-0.5, maxval=0.5)
    chan_scale = 10.0 ** jax.random.uniform(chan_key, (1, 1, 1, LEV * C), minval=-0.5, maxval=0.5)
    noise = jnp.clip(jax.random.normal(noise_key, shape), -4.0, 4.0)
    return (noise * ramp * lat_scale * chan_scale).astype(jnp.bfloat16)


def draw_bias_table(key, part):
    base_key = jax.random.fold_in(key, 0)
    shape = (WTYPES, NPOS, HEADS)
    table = 0.5 * jnp.clip(jax.random.normal(base_key, shape), -4.0, 4.0)
    return table


def place_ends(drawn, key, smallest, largest):
    longest = drawn.shape.index(max(drawn.shape))
    spots = []
    for shift in (0, 1):
        where = [jax.random.randint(jax.random.fold_in(key, axis), (), 0, length) for axis, length in enumerate(drawn.shape)]
        where[longest] = (where[longest] + shift) % drawn.shape[longest]
        spots.append(tuple(where))
    return drawn.at[spots[0]].set(smallest).at[spots[1]].set(largest)


def block_scale(own_key, dims, pieces, smallest, high):
    def one(dim, shards_of):
        heights = jax.random.uniform(jax.random.fold_in(jax.random.fold_in(own_key, 6), dim), (shards_of,), jnp.float32, smallest / len(pieces), high / len(pieces))
        return jnp.repeat(jnp.exp(heights), dims[dim] // shards_of).reshape((-1,) + (1,) * (len(dims) - dim - 1))

    gain = one(*pieces[0])
    for cut in pieces[1:]:
        gain = gain * one(*cut)
    return gain


def normal_values(own_key, shape, deviation, reach, cuts=(), kind=jnp.bfloat16):
    drawn = jax.random.normal(own_key, shape, jnp.float32) * deviation
    if len(cuts) > 0:
        drawn = block_scale(own_key, shape, cuts, -0.22, 0.18) * drawn
    return jnp.clip(drawn, min=-reach, max=reach).astype(kind)


def setup_inputs(seed: int = 0, part: int = 0) -> dict:
    arg_keys = jax.random.split(jax.random.key(seed), 11)
    part_keys = jax.random.split(jax.random.fold_in(arg_keys[10], part), 11)
    return {
        "base_state": normal_values(part_keys[0], (LON, LAT, LEV * C), 1.0, 6.0, ((0, 16),)),
        "tangents": draw_tangents(jax.random.fold_in(jax.random.fold_in(arg_keys[10], part), 71), part),
        "norm_gain": jnp.clip(1.0 + 0.15 * jax.random.normal(arg_keys[2], (C,), jnp.float32), 0.25, 1.75),
        "qkv_weight": normal_values(arg_keys[3], (C, 3 * C), C ** -0.5, 0.4375),
        "out_weight": normal_values(arg_keys[4], (C, C), C ** -0.5, 0.4375),
        "bias_table": draw_bias_table(jax.random.fold_in(arg_keys[10], 71), part),
        "bias_index": place_ends(jax.random.randint(arg_keys[6], (WLON * WLAT * WLEV, WLON * WLAT * WLEV), 0, NPOS), jax.random.fold_in(arg_keys[6], 1), 0, NPOS - 1).astype(jnp.int32),
        "region": place_ends(jax.random.randint(arg_keys[7], (LAT, LEV), 0, 3), jax.random.fold_in(arg_keys[7], 1), 0, 2).astype(jnp.int32),
        "energy_table": jnp.clip(jnp.exp(jax.random.uniform(arg_keys[8], (ECLS, C), jnp.float32, math.log(0.3), math.log(3.0))), 0.3, 3.0),
        "level_class": place_ends(jax.random.randint(arg_keys[9], (LEV,), 0, ECLS), jax.random.fold_in(arg_keys[9], 1), 0, ECLS - 1).astype(jnp.int32),
    }


def build_tables(bias_table, bias_index, region):
    bias_full = jnp.transpose(bias_table[:, bias_index, :], (0, 3, 1, 2))
    window_ids = region.reshape(LAT // WLAT, WLAT, LEV // WLEV, WLEV).transpose(0, 2, 1, 3)
    window_ids = window_ids.reshape(WTYPES, 1, WLAT * WLEV)
    window_ids = jnp.broadcast_to(window_ids, (WTYPES, WLON, WLAT * WLEV)).reshape(WTYPES, WLON * WLAT * WLEV)
    allowed = window_ids[:, :, None] == window_ids[:, None, :]
    return (bias_full, allowed)

def energy_weights(energy_table, level_class):
    one_hot = level_class[:, None] == jnp.arange(ECLS, dtype=jnp.int32)[None, :]
    picked = lax.optimization_barrier(jnp.sum(jnp.where(one_hot[:, :, None], energy_table[None], 0.0), axis=1))
    return picked.reshape(LEV * C)

def attend(field_in, norm_gain, qkv_weight, out_weight, bias_full, allowed):
    window_count = field_in.shape[0] // WLON
    window_size = WLON * WLAT * WLEV
    grid_view = field_in.reshape(window_count, WLON, LAT // WLAT, WLAT, LEV // WLEV, WLEV, C)
    token_rows = grid_view.transpose(0, 2, 4, 1, 3, 5, 6).reshape(window_count, WTYPES, window_size, C)
    centered = token_rows - lax.optimization_barrier(jnp.mean(token_rows, -1, keepdims=True))
    variance = lax.optimization_barrier(jnp.mean(centered * centered, -1, keepdims=True))
    normed = (centered * lax.rsqrt(variance + 1e-05) * norm_gain).astype(jnp.bfloat16)
    packed = jnp.einsum('mwtc,cd->mwtd', normed.astype(jnp.float32), qkv_weight.astype(jnp.float32)).astype(jnp.bfloat16)
    packed = packed.reshape(window_count, WTYPES, window_size, 3, HEADS, HEAD)
    query_rows = packed[:, :, :, 0].astype(jnp.float32)
    key_rows = packed[:, :, :, 1].astype(jnp.float32)
    value_rows = packed[:, :, :, 2].astype(jnp.float32)
    scores = jnp.einsum('mwqhd,mwkhd->mwhqk', query_rows, key_rows) * HEAD ** (-0.5) + bias_full[None]
    scores = jnp.where(allowed[None, :, None], scores, -1000000000.0)
    peak_score = lax.stop_gradient(lax.optimization_barrier(jnp.max(scores, -1, keepdims=True)))
    raised = jnp.exp(scores - peak_score)
    weights = (raised / lax.optimization_barrier(jnp.sum(raised, -1, keepdims=True))).astype(jnp.bfloat16)
    blended = jnp.einsum('mwhqk,mwkhd->mwqhd', weights.astype(jnp.float32), value_rows).astype(jnp.bfloat16)
    blended = blended.reshape(window_count, WTYPES, window_size, C)
    result = jnp.einsum('mwtc,cd->mwtd', blended.astype(jnp.float32), out_weight.astype(jnp.float32))
    result = result.reshape(window_count, LAT // WLAT, LEV // WLEV, WLON, WLAT, WLEV, C)
    return result.transpose(0, 3, 1, 4, 2, 5, 6).reshape(field_in.shape)

def linear_parts(apply_fn, point):
    output, pull_back = jax.vjp(apply_fn, point)

    def backward_map(cotangent):
        return pull_back(cotangent)[0]

    def forward_map(tangent):
        empty_out = jnp.zeros_like(output)
        unused, transposed = jax.vjp(backward_map, empty_out)
        return transposed(tangent)[0]
    return (forward_map, backward_map)

def reference(base_state, tangents, norm_gain, qkv_weight, out_weight, bias_table, bias_index, region, energy_table, level_class):
    bias_full, allowed = build_tables(bias_table, bias_index, region)
    energy = energy_weights(energy_table, level_class)
    half_window = WLON // 2

    def block_branch(field_in):
        rolled = jnp.roll(field_in, -half_window, 0)
        return jnp.roll(attend(rolled, norm_gain, qkv_weight, out_weight, bias_full, allowed), half_window, 0)
    forward_map, backward_map = linear_parts(block_branch, base_state.astype(jnp.float32))
    directions = tangents.astype(jnp.float32)
    images = directions + lax.map(forward_map, directions)
    weighted = energy * images
    gradients = weighted + lax.map(backward_map, weighted)
    scaled = gradients / energy
    total = float(LON * LAT * LEV * C)
    first_sum = jnp.sum(energy * scaled[0] * scaled[0])
    first = scaled[0] * jnp.sqrt(total / first_sum)
    cross_term = jnp.sum(energy * scaled[1] * first)
    second = scaled[1] - cross_term / total * first
    second_sum = jnp.sum(energy * second * second)
    return jnp.stack([first, second * jnp.sqrt(total / second_sum)])
```

```python
import functools

import jax
import jax.numpy as jnp
from jax import lax
from jax.experimental import pallas as pl
from jax.experimental.pallas import tpu as pltpu
from jax.sharding import PartitionSpec as P

C = 192
HEADS = 6
HEAD = 32
WLON = 12
WLAT = 6
WLEV = 2
LEV = 4
ECLS = 3
LAT = 6
WTYPES = 2
NPOS = 3312

HALF = WLON // 2
TOK = WLON * WLAT * WLEV
PLANE = WLON * WLAT
LANE = 128
TAIL = TOK - LANE
WIDE = 2 * LANE
KEYS = (HEADS + 1) * LANE
ROWS = -(-NPOS // LANE)
NEG = -1000000000.0


def iota(shape, dim):
    return lax.broadcasted_iota(jnp.int32, shape, dim)


def dot(a, b):
    return lax.dot_general(a, b, (((1,), (0,)), ((), ())), preferred_element_type=jnp.float32)


def dot_nt(a, b):
    return lax.dot_general(a, b, (((1,), (1,)), ((), ())), preferred_element_type=jnp.float32)


def dot_tn(a, b):
    return lax.dot_general(a, b, (((0,), (0,)), ((), ())), preferred_element_type=jnp.float32)


def bias_kernel(region, idx_ref, tab_ref, out_ref, hi_ref, lo_ref):
    row, col = iota((TOK, TOK), 0), iota((TOK, TOK), 1)
    rows = ((row % PLANE) * WLEV + row // PLANE == col).astype(jnp.bfloat16)
    row, col = iota((TOK, WIDE), 0), iota((TOK, WIDE), 1)
    key = jnp.where(col < LANE, col, LANE + col % TAIL)
    cols = ((key % PLANE) * WLEV + key // PLANE == row).astype(jnp.bfloat16)

    def ordered(value):
        value = value.astype(jnp.float32).astype(jnp.bfloat16)
        return dot(dot(rows, value).astype(jnp.bfloat16), cols).astype(jnp.int32)

    idx = idx_ref[...]
    high, low = ordered(idx >> 7), ordered(idx & 127)
    hi_ref[0:TOK, :] = high[:, :LANE]
    lo_ref[0:TOK, :] = low[:, :LANE]
    slot = iota((8, LANE), 1) // TAIL
    for pack in range(-(-TOK // 64)):
        h = jnp.zeros((8, LANE), jnp.int32)
        l = jnp.zeros((8, LANE), jnp.int32)
        for u in range(8):
            at = 64 * pack + 8 * u
            if at < TOK:
                h = jnp.where(slot == u, high[at : at + 8, LANE:], h)
                l = jnp.where(slot == u, low[at : at + 8, LANE:], l)
        hi_ref[TOK + 8 * pack : TOK + 8 * pack + 8, :] = h
        lo_ref[TOK + 8 * pack : TOK + 8 * pack + 8, :] = l

    def gathered(at):
        h, l = hi_ref[pl.ds(at, 8), :], lo_ref[pl.ds(at, 8), :]
        found = [jnp.zeros((8, LANE), jnp.float32) for _ in range(WTYPES * HEADS)]
        for b in range(ROWS):
            here = h == b
            for n in range(WTYPES * HEADS):
                source = jnp.broadcast_to(tab_ref[n, b : b + 1, :], (8, LANE))
                found[n] = jnp.where(here, jnp.take_along_axis(source, l, axis=1), found[n])
        return found

    def regions(token, t):
        level, lat = token // PLANE, token % WLAT
        found = jnp.zeros(token.shape, jnp.int32)
        for l in range(WLEV):
            for j in range(WLAT):
                found = jnp.where((level == l) & (lat == j), region[j, WLEV * t + l], found)
        return found

    lane = iota((8, LANE), 1)
    key_main = [regions(lane, t) for t in range(WTYPES)]
    key_tail = [regions(LANE + lane % TAIL, t) for t in range(WTYPES)]

    def main_rows(g, _):
        at = pl.multiple_of(g * 8, 8)
        found = gathered(at)
        query = iota((8, LANE), 0) + at
        for t in range(WTYPES):
            ok = regions(query, t) == key_main[t]
            for h in range(HEADS):
                out_ref[t, pl.ds(at, 8), LANE * h : LANE * (h + 1)] = jnp.where(ok, found[t * HEADS + h], NEG)
        return 0

    lax.fori_loop(0, TOK // 8, main_rows, 0)
    for pack in range(-(-TOK // 64)):
        found = gathered(TOK + 8 * pack)
        for u in range(8):
            at = 64 * pack + 8 * u
            if at >= TOK:
                break
            query = iota((8, LANE), 0) + at
            for t in range(WTYPES):
                ok = (regions(query, t) == key_tail[t]) & (slot < HEADS)
                value = jnp.full((8, LANE), NEG, jnp.float32)
                for h in range(HEADS):
                    moved = pltpu.roll(found[t * HEADS + h], (TAIL * (h - u)) % LANE, 1)
                    value = jnp.where(slot == h, moved, value)
                out_ref[t, at : at + 8, LANE * HEADS :] = jnp.where(ok, value, NEG)


def window_kernel(classes, x_ref, gain_ref, w_ref, out_w_ref, bias_ref, table_ref, scaled_ref, sums_ref):
    f32, bf16 = jnp.float32, jnp.bfloat16
    gain = gain_ref[...]
    wq, wk, wv = (w_ref[:, WIDE * n : WIDE * (n + 1)] for n in range(3))
    wo = out_w_ref[...]
    scale = HEAD ** (-0.5)
    table = table_ref[...]

    def energy_row(level):
        found = jnp.zeros((1, C), f32)
        for e in range(ECLS):
            found = found + jnp.where(classes[level] == e, table[e : e + 1, :], 0.0)
        return found

    lane = iota((1, WIDE), 1)
    head_of = jnp.where(lane < C, lane // HEAD, -1)
    row, col = iota((WIDE, WIDE), 0), iota((WIDE, WIDE), 1)
    spread = ((row < C) & (col >= C) & ((col - C) % 32 == row // HEAD)).astype(bf16)

    def by_head(value, ones):
        main, tail = [], []
        for h in range(HEADS):
            keep = head_of == h
            rest = jnp.zeros((1, WIDE), bf16)
            if ones:
                rest = ((lane == C + h) | (lane == C + 32 + h)).astype(bf16)
            main.append(jnp.where(keep, value[:LANE], rest))
            tail.append(jnp.where(keep, value[LANE:], rest))
        filler = jnp.zeros((KEYS - HEADS * TOK, WIDE), bf16)
        return jnp.concatenate(main + tail + [filler], 0)

    def with_shift(value, product):
        high = product.astype(bf16)
        low = (product - high.astype(f32)).astype(bf16)
        sums = dot(high, spread) + dot(low, spread)
        top = sums.astype(bf16)
        rest = (sums - top.astype(f32)).astype(bf16)
        return jnp.where(lane < C, value, jnp.where(lane < C + 32, -top, -rest))

    def transposed_product(left_t, ds):
        main = []
        for j in range(HEADS // 2):
            part = dot(left_t[64 * j : 64 * j + 64], ds[:, WIDE * j : WIDE * (j + 1)])
            main += [part[:HEAD, :LANE], part[HEAD:, LANE:]]
        last = dot(left_t[:C], ds[:, LANE * HEADS :])
        tail = []
        for h in range(HEADS):
            block = last[HEAD * h : HEAD * (h + 1)]
            tail.append(pltpu.roll(block, (LANE - TAIL * h) % LANE, 1)[:, :TAIL])
        return jnp.concatenate([jnp.concatenate(main, 0), jnp.concatenate(tail, 0)], 1)

    slot = iota((TOK, LANE), 1) // TAIL
    totals = [jnp.zeros((1, C), f32) for _ in range(3)]
    for t in range(WTYPES):
        def tokens(field):
            parts = [
                x_ref[0, field, :, C * l : C * (l + 1)].astype(f32)
                for l in range(WLEV * t, WLEV * (t + 1))
            ]
            return jnp.concatenate(parts, 0)

        base = tokens(0)
        centered = base - jnp.mean(base, -1, keepdims=True)
        rstd = lax.rsqrt(jnp.mean(centered * centered, -1, keepdims=True) + 1e-05)
        hat = centered * rstd
        normed = (hat * gain).astype(bf16)
        q, k, v = (dot(normed, w).astype(bf16) for w in (wq, wk, wv))
        k_heads, v_heads = by_head(k, True), by_head(v, True)

        scores = dot_nt(q, k_heads) * scale + bias_ref[t]
        tails = scores[:, LANE * HEADS :]
        raised, sums = [], []
        tail_peak = jnp.zeros((TOK, LANE), f32)
        for h in range(HEADS):
            main = scores[:, LANE * h : LANE * (h + 1)]
            peak = jnp.max(jnp.maximum(main, jnp.where(slot == h, tails, -jnp.inf)), -1, keepdims=True)
            raised.append(jnp.exp(main - peak))
            tail_peak = jnp.where(slot == h, peak, tail_peak)
        tails = jnp.exp(tails - tail_peak)
        tail_inv = jnp.zeros((TOK, LANE), f32)
        for h in range(HEADS):
            inv = 1.0 / jnp.sum(raised[h] + jnp.where(slot == h, tails, 0.0), -1, keepdims=True)
            raised[h] = raised[h] * inv
            tail_inv = jnp.where(slot == h, inv, tail_inv)
        probs = jnp.concatenate(raised + [tails * tail_inv], 1)
        weights = probs.astype(bf16)
        probs = probs * scale
        mean_v = dot(weights, v_heads)
        mean_k = dot(weights, k_heads)
        q_t = q.astype(f32).T.astype(bf16)

        def energy_rows():
            rows = [energy_row(WLEV * t + l) for l in range(WLEV)]
            return jnp.concatenate([jnp.broadcast_to(r, (PLANE, C)) for r in rows], 0)

        energy = energy_rows()
        result = []
        for f in range(2):
            direction = tokens(1 + f)
            moved = direction - jnp.mean(direction, -1, keepdims=True) - hat * jnp.mean(hat * direction, -1, keepdims=True)
            moved = (moved * rstd * gain).astype(bf16)
            dq, dk, dv = (dot(moved, w).astype(bf16) for w in (wq, wk, wv))
            dk_heads, dv_heads = by_head(dk, False), by_head(dv, False)
            mean_dk = dot(weights, dk_heads)
            mean_dv = dot(weights, dv_heads)
            shifted = with_shift(dq, dq.astype(f32) * mean_k + q.astype(f32) * mean_dk)
            dscores = dot_nt(shifted, k_heads) + dot_nt(q, dk_heads)
            dweights = (probs * dscores).astype(bf16)
            dblended = (dot(dweights, v_heads) + mean_dv).astype(bf16)
            image = direction + dot(dblended[:, :C], wo)

            cot = dot_nt((energy * image).astype(bf16), wo).astype(bf16)
            cot = jnp.concatenate([cot, jnp.zeros((TOK, WIDE - C), bf16)], 1)
            shifted = with_shift(cot, cot.astype(f32) * mean_v)
            cscores = (probs * dot_nt(shifted, v_heads)).astype(bf16)
            cq = dot(cscores, k_heads).astype(bf16)
            ck_t = transposed_product(q_t, cscores).astype(bf16)
            cv_t = transposed_product(cot.astype(f32).T.astype(bf16), weights).astype(bf16)
            cnormed = dot_nt(cq, wq) + dot_tn(ck_t, wk.T[:C]) + dot_tn(cv_t, wv.T[:C])
            cnormed = cnormed.astype(bf16).astype(f32) * gain
            back = cnormed - jnp.mean(cnormed, -1, keepdims=True) - hat * jnp.mean(hat * cnormed, -1, keepdims=True)
            out = image + back * rstd / energy
            result.append(out)
            for l in range(WLEV):
                at = WLEV * t + l
                scaled_ref[0, f, :, C * at : C * (at + 1)] = out[PLANE * l : PLANE * (l + 1)]
        for n, (a, b) in enumerate(((0, 0), (0, 1), (1, 1))):
            totals[n] = totals[n] + jnp.sum(energy * result[a] * result[b], 0, keepdims=True)
    lane = iota((1, LANE), 1)
    found = jnp.zeros((1, LANE), f32)
    for n in range(3):
        found = jnp.where(lane == n, jnp.sum(totals[n], -1, keepdims=True), found)
    sums_ref[0] = jnp.broadcast_to(found, (8, LANE))


def whole(memory=pltpu.VMEM):
    return pl.BlockSpec(memory_space=memory)


def pair_bias(bias_table, bias_index, region):
    table = jnp.transpose(bias_table, (0, 2, 1)).reshape(WTYPES * HEADS, NPOS)
    table = jnp.pad(table, ((0, 0), (0, ROWS * LANE - NPOS))).reshape(WTYPES * HEADS, ROWS, LANE)
    packs = TOK + 8 * -(-TOK // 64)
    return pl.pallas_call(
        bias_kernel,
        out_shape=jax.ShapeDtypeStruct((WTYPES, TOK, KEYS), jnp.float32),
        in_specs=[whole(pltpu.SMEM), whole(), whole()],
        out_specs=whole(),
        scratch_shapes=[pltpu.VMEM((packs, LANE), jnp.int32)] * 2,
        cost_estimate=pl.CostEstimate(flops=100000000, bytes_accessed=1400000, transcendentals=0),
        name="pair_bias",
    )(region, bias_index, table)


def windows(fields, gain, weight, out_weight, bias, energy_table, level_class):
    count = fields.shape[0]

    def fixed(shape):
        return pl.BlockSpec(shape, lambda n: (0,) * len(shape))

    def moving(shape):
        return pl.BlockSpec((1,) + shape[1:], lambda n: (n,) + (0,) * (len(shape) - 1))

    outs = [(count, 2, PLANE, LEV * C), (count, 8, LANE)]
    return pl.pallas_call(
        window_kernel,
        grid=(count,),
        out_shape=[jax.ShapeDtypeStruct(s, jnp.float32) for s in outs],
        in_specs=[
            whole(pltpu.SMEM),
            moving(fields.shape),
            fixed(gain.shape),
            fixed(weight.shape),
            fixed(out_weight.shape),
            fixed(bias.shape),
            fixed(energy_table.shape),
        ],
        out_specs=[moving(s) for s in outs],
        compiler_params=pltpu.CompilerParams(vmem_limit_bytes=48 * 1024 * 1024),
        cost_estimate=pl.CostEstimate(flops=2000000000, bytes_accessed=2500000, transcendentals=250000),
        name="window_step",
    )(level_class, fields, gain, weight, out_weight, bias, energy_table)


def summed(value, axis):
    size = lax.axis_size(axis)
    if size & (size - 1):
        return lax.psum(value, axis)
    step = 1
    while step < size:
        value = value + lax.ppermute(value, axis, [(i, i ^ step) for i in range(size)])
        step *= 2
    return value


def local(
    base_state,
    tangents,
    norm_gain,
    qkv_weight,
    out_weight,
    bias_table,
    bias_index,
    region,
    energy_table,
    level_class,
):
    columns = base_state.shape[0]
    size = lax.axis_size("lon")
    count = columns // WLON
    up = [(i, (i + 1) % size) for i in range(size)]
    down = [(j, i) for i, j in up]
    fields = jnp.concatenate([base_state[None], tangents], 0).reshape(3, columns * LAT, LEV * C)
    edge = HALF * LAT
    arrived = lax.ppermute(fields[:, :edge], "lon", down)
    bias = pair_bias(bias_table, bias_index, region)
    weight = jnp.pad(qkv_weight.reshape(C, 3, C), ((0, 0), (0, 0), (0, WIDE - C))).reshape(C, 3 * WIDE)
    shifted = jnp.concatenate([fields[:, edge:], arrived], 1)
    shifted = shifted.reshape(3, count, PLANE, LEV * C).swapaxes(0, 1)
    scaled, sums = windows(shifted, norm_gain[None], weight, out_weight, bias, energy_table, level_class)
    scaled = scaled.swapaxes(0, 1).reshape(2, columns * LAT, LEV * C)
    entries = jnp.sum(sums[:, 0, :], 0)
    kept = columns * LAT - edge
    returned = lax.ppermute(scaled[:, kept:].astype(jnp.bfloat16), "lon", up)
    entries = summed(entries, "lon")
    scaled = jnp.concatenate([returned.astype(jnp.float32), scaled[:, :kept]], 1)
    scaled = scaled.reshape(2, columns, LAT, LEV * C)
    total = float(columns * size * LAT * LEV * C)
    first = scaled[0] * jnp.sqrt(total / entries[0])
    second = scaled[1] - entries[1] / entries[0] * scaled[0]
    second_sum = entries[2] - entries[1] * entries[1] / entries[0]
    return jnp.stack([first, second * jnp.sqrt(total / second_sum)])


def solution(mesh):
    placed = (
        P(("grp", "lon"), None, None),
        P(None, ("grp", "lon"), None, None),
    ) + (P(),) * 8
    return jax.shard_map(
        local,
        mesh=mesh,
        in_specs=placed,
        out_specs=P(None, ("grp", "lon"), None, None),
        check_vma=False,
    )
```

```python
import functools

import jax
import jax.numpy as jnp
from jax import lax
from jax.experimental import pallas as pl
from jax.experimental.pallas import tpu as pltpu
from jax.sharding import PartitionSpec as P

C = 192
HEADS = 6
HEAD = 32
WLON = 12
WLAT = 6
WLEV = 2
LEV = 4
ECLS = 3
LAT = 6
WTYPES = 2
NPOS = 3312

HALF = WLON // 2
TOK = WLON * WLAT * WLEV
PLANE = WLON * WLAT
LANE = 128
TAIL = TOK - LANE
WIDE = 2 * LANE
KEYS = (HEADS + 1) * LANE
ROWS = -(-NPOS // LANE)
NEG = -1000000000.0

HI_PAIR = 0
TAIL_AT = WIDE
MAIN_AT = WIDE + LANE
SMALLEST, LARGEST = -2.0, 306.0
STEPS = 65535.0


def main_at(h):
    return MAIN_AT + LANE * h if h < 4 else HI_PAIR + LANE * (h - 4)


def iota(shape, dim):
    return lax.broadcasted_iota(jnp.int32, shape, dim)


def dot(a, b):
    return lax.dot_general(a, b, (((1,), (0,)), ((), ())), preferred_element_type=jnp.float32)


def dot_nt(a, b):
    return lax.dot_general(a, b, (((1,), (1,)), ((), ())), preferred_element_type=jnp.float32)


def dot_tn(a, b):
    return lax.dot_general(a, b, (((0,), (0,)), ((), ())), preferred_element_type=jnp.float32)


def prepare_kernel(region, idx_ref, tab_ref, w_ref, bias_ref, wide_ref, hi_ref, lo_ref, pair_ref):
    weight = w_ref[...].astype(jnp.float32)
    for n in range(3):
        part = jnp.concatenate([weight[:, C * n : C * (n + 1)], jnp.zeros((C, WIDE - C), jnp.float32)], 1)
        wide_ref[:, WIDE * n : WIDE * (n + 1)] = part.astype(jnp.bfloat16)

    step = (LARGEST - SMALLEST) / STEPS

    def steps(value):
        value = jnp.clip((value - SMALLEST) * (1.0 / step), 0.0, STEPS)
        return (value + 0.5).astype(jnp.int32)

    pair_ref[:, NPOS // LANE * LANE :] = jnp.zeros((8, LANE), jnp.int32)
    pair_ref[0:HEADS, 0:NPOS] = steps(tab_ref[:, 0, :]) * 65536 + steps(tab_ref[:, 1, :])

    def values(word):
        top = lax.shift_right_logical(word, 16).astype(jnp.float32)
        low = (word & 65535).astype(jnp.float32)
        return top * step + SMALLEST, low * step + SMALLEST

    row, col = iota((TOK, TOK), 0), iota((TOK, TOK), 1)
    rows = ((row % PLANE) * WLEV + row // PLANE == col).astype(jnp.bfloat16)
    row, col = iota((TOK, WIDE), 0), iota((TOK, WIDE), 1)
    key = jnp.where(col < LANE, col, LANE + col % TAIL)
    cols = ((key % PLANE) * WLEV + key // PLANE == row).astype(jnp.bfloat16)

    def ordered(value):
        value = value.astype(jnp.float32).astype(jnp.bfloat16)
        return dot(dot(rows, value).astype(jnp.bfloat16), cols).astype(jnp.int32)

    idx = idx_ref[...]
    high, low = ordered(idx >> 7), ordered(idx & 127)
    hi_ref[0:TOK, :] = high[:, :LANE]
    lo_ref[0:TOK, :] = low[:, :LANE]
    slot = iota((8, LANE), 1) // TAIL
    for pack in range(-(-TOK // 64)):
        h = jnp.zeros((8, LANE), jnp.int32)
        l = jnp.zeros((8, LANE), jnp.int32)
        for u in range(8):
            at = 64 * pack + 8 * u
            if at < TOK:
                h = jnp.where(slot == u, high[at : at + 8, LANE:], h)
                l = jnp.where(slot == u, low[at : at + 8, LANE:], l)
        hi_ref[TOK + 8 * pack : TOK + 8 * pack + 8, :] = h
        lo_ref[TOK + 8 * pack : TOK + 8 * pack + 8, :] = l

    def gathered(at):
        h, l = hi_ref[pl.ds(at, 8), :], lo_ref[pl.ds(at, 8), :]
        found = [jnp.zeros((8, LANE), jnp.int32) for _ in range(HEADS)]
        for b in range(ROWS):
            here = h == b
            for n in range(HEADS):
                source = jnp.broadcast_to(pair_ref[n : n + 1, LANE * b : LANE * (b + 1)], (8, LANE))
                found[n] = jnp.where(here, jnp.take_along_axis(source, l, axis=1), found[n])
        return [values(f) for f in found]

    def regions(token, t):
        level, lat = token // PLANE, token % WLAT
        found = jnp.zeros(token.shape, jnp.int32)
        for l in range(WLEV):
            for j in range(WLAT):
                found = jnp.where((level == l) & (lat == j), region[WLEV * t + l, j], found)
        return found

    lane = iota((8, LANE), 1)
    key_main = [regions(lane, t) for t in range(WTYPES)]
    key_tail = [regions(LANE + lane % TAIL, t) for t in range(WTYPES)]

    def main_rows(g, _):
        at = pl.multiple_of(g * 8, 8)
        found = gathered(at)
        query = iota((8, LANE), 0) + at
        for t in range(WTYPES):
            ok = regions(query, t) == key_main[t]
            for h in range(HEADS):
                bias_ref[t, pl.ds(at, 8), main_at(h) : main_at(h) + LANE] = jnp.where(ok, found[h][t], NEG)
        return 0

    lax.fori_loop(0, TOK // 8, main_rows, 0)
    for pack in range(-(-TOK // 64)):
        found = gathered(TOK + 8 * pack)
        for u in range(8):
            at = 64 * pack + 8 * u
            if at >= TOK:
                break
            query = iota((8, LANE), 0) + at
            for t in range(WTYPES):
                ok = (regions(query, t) == key_tail[t]) & (slot < HEADS)
                value = jnp.full((8, LANE), NEG, jnp.float32)
                for h in range(HEADS):
                    moved = pltpu.roll(found[h][t], (TAIL * (h - u)) % LANE, 1)
                    value = jnp.where(slot == h, moved, value)
                bias_ref[t, at : at + 8, TAIL_AT:MAIN_AT] = jnp.where(ok, value, NEG)


def window_kernel(classes, x_ref, gain_ref, w_ref, out_w_ref, bias_ref, table_ref, scaled_ref, back_ref, sums_ref):
    f32, bf16 = jnp.float32, jnp.bfloat16

    def padded(row):
        return jnp.concatenate([row, jnp.zeros((row.shape[0], WIDE - C), row.dtype)], 1)

    gain = padded(gain_ref[...])
    wq, wk, wv = (w_ref[:, WIDE * n : WIDE * (n + 1)] for n in range(3))
    wk_t, wv_t = wk.T[:C], wv.T[:C]
    wo = out_w_ref[...]
    wo = jnp.concatenate([wo.astype(f32), jnp.zeros((C, WIDE - C), f32)], 1).astype(bf16)
    scale = HEAD ** (-0.5)
    table = table_ref[...]

    def energy_row(level):
        found = jnp.zeros((1, C), f32)
        for e in range(ECLS):
            found = found + jnp.where(classes[level] == e, table[e : e + 1, :], 0.0)
        return found

    lane = iota((1, LANE), 1)
    extra = lane >= C - LANE
    row, col = iota((WIDE, LANE), 0), iota((WIDE, LANE), 1)
    spread = ((row < C) & (col >= C - LANE) & (col % 32 == row // HEAD)).astype(bf16)
    row, col = iota((4 * LANE, LANE), 0), iota((4 * LANE, LANE), 1)
    marks = ((col >= C - LANE) & (col % 32 == row // LANE)).astype(bf16)

    def by_head(value, ones):
        low, high = value[:, :LANE], value[:, LANE:]
        nothing = jnp.zeros((1, LANE), bf16)
        left, right, left_tail, right_tail = [], [], [], []
        for h in range(HEADS):
            mark = (extra & (lane % 32 == h)).astype(bf16) if ones else nothing
            if h < 4:
                keep = lane // HEAD == h
                left.append(jnp.where(keep, low[:LANE], nothing))
                left_tail.append(jnp.where(keep, low[LANE:], nothing))
                right_tail.append(jnp.broadcast_to(mark, (TAIL, LANE)))
            else:
                keep = lane // HEAD == h - 4
                right.append(jnp.where(keep, high[:LANE], mark))
                right_tail.append(jnp.where(keep, high[LANE:], mark))
        left_tail.append(jnp.zeros((LANE - 4 * TAIL, LANE), bf16))
        right_tail.append(jnp.zeros((LANE - HEADS * TAIL, LANE), bf16))
        return jnp.concatenate(left_tail + left, 0), jnp.concatenate(right + right_tail, 0)

    def against(a, heads, marked):
        left, right = heads
        parts = [
            dot_nt(a[:, LANE:], right[:WIDE]),
            dot_nt(a, jnp.concatenate([left[:LANE], right[WIDE:]], 1)),
        ]
        if marked:
            parts.append(dot_nt(a, jnp.concatenate([left[LANE:], marks], 1)))
        else:
            parts.append(dot_nt(a[:, :LANE], left[LANE:]))
        return jnp.concatenate(parts, 1)

    def mixed(w, *heads):
        left = dot(w[:, TAIL_AT:], jnp.concatenate([h[0] for h in heads], 1))
        right = dot(w[:, :MAIN_AT], jnp.concatenate([h[1] for h in heads], 1))
        found = []
        for n in range(len(heads)):
            at = slice(LANE * n, LANE * (n + 1))
            found.append(jnp.concatenate([left[:, at], right[:, at]], 1))
        return found

    def with_shift(value, product):
        sums = dot(product.astype(bf16), spread)
        top = sums.astype(bf16)
        rest = (sums - top.astype(f32)).astype(bf16)
        last = jnp.where(extra, jnp.where(lane < 96, -top, -rest), value[:, LANE:])
        return jnp.concatenate([value[:, :LANE], last], 1)

    def pair_columns(j):
        return slice(MAIN_AT + WIDE * j, MAIN_AT + WIDE * (j + 1)) if j < 2 else slice(HI_PAIR, WIDE)

    def transposed_product(lefts, ds):
        count = len(lefts)
        main = [[] for _ in lefts]
        for j in range(HEADS // 2):
            stacked = jnp.concatenate([l[64 * j : 64 * j + 64] for l in lefts], 0)
            part = dot(stacked, ds[:, pair_columns(j)])
            for n in range(count):
                main[n] += [part[64 * n : 64 * n + 32, :LANE], part[64 * n + 32 : 64 * n + 64, LANE:]]
        last = dot(jnp.concatenate([l[:C] for l in lefts], 0), ds[:, TAIL_AT:MAIN_AT])
        found = []
        for n in range(count):
            tail = []
            for h in range(HEADS):
                block = last[C * n + HEAD * h : C * n + HEAD * (h + 1)]
                tail.append(pltpu.roll(block, (LANE - TAIL * h) % LANE, 1)[:, :TAIL])
            both = [jnp.concatenate(main[n], 0), jnp.concatenate(tail, 0)]
            found.append(jnp.concatenate(both, 1).astype(bf16))
        return found

    def turned(value):
        return value.astype(f32).T.astype(bf16)

    def mean(value):
        return jnp.sum(value, -1, keepdims=True) * (1.0 / C)

    channel = iota((1, WIDE), 1) < C
    slot = iota((TOK, LANE), 1) // TAIL
    totals = [jnp.zeros((1, WIDE), f32) for _ in range(3)]
    for t in range(WTYPES):

        def tokens(field):
            parts = []
            for l in range(WLEV * t, WLEV * (t + 1)):
                start = C * l // LANE * LANE
                part = x_ref[field, :, start : start + WIDE].astype(f32)
                if start < C * l:
                    part = pltpu.roll(part, WIDE - (C * l - start), 1)
                parts.append(jnp.where(channel, part, 0.0))
            return jnp.concatenate(parts, 0)

        base = tokens(0)
        centered = jnp.where(channel, base - mean(base), 0.0)
        rstd = lax.rsqrt(mean(centered * centered) + 1e-05)
        hat = centered * rstd
        normed = (hat * gain).astype(bf16)[:, :C]
        q, k, v = (dot(normed, w).astype(bf16) for w in (wq, wk, wv))
        k_heads, v_heads = by_head(k, True), by_head(v, True)

        scores = against(q, k_heads, False) * scale + bias_ref[t]
        tails = scores[:, TAIL_AT:MAIN_AT]
        raised = []
        tail_peak = jnp.zeros((TOK, LANE), f32)
        for h in range(HEADS):
            main = scores[:, main_at(h) : main_at(h) + LANE]
            peak = jnp.max(jnp.maximum(main, jnp.where(slot == h, tails, -jnp.inf)), -1, keepdims=True)
            raised.append(jnp.exp(main - peak))
            tail_peak = jnp.where(slot == h, peak, tail_peak)
        tails = jnp.exp(tails - tail_peak)
        tail_inv = jnp.zeros((TOK, LANE), f32)
        for h in range(HEADS):
            inv = 1.0 / jnp.sum(raised[h] + jnp.where(slot == h, tails, 0.0), -1, keepdims=True)
            raised[h] = raised[h] * inv
            tail_inv = jnp.where(slot == h, inv, tail_inv)
        probs = jnp.concatenate(raised[4:] + [tails * tail_inv] + raised[:4], 1)
        weights = probs.astype(bf16)
        probs = probs * scale
        mean_v, mean_k = mixed(weights, v_heads, k_heads)
        q_t = turned(q)

        rows = [energy_row(WLEV * t + l) for l in range(WLEV)]
        energy = jnp.concatenate([jnp.broadcast_to(padded(r), (PLANE, WIDE)) for r in rows], 0)
        inverse = jnp.concatenate([jnp.broadcast_to(padded(1.0 / r), (PLANE, WIDE)) for r in rows], 0)

        def both(value):
            return jnp.concatenate([value, value], 0)

        direction = jnp.concatenate([tokens(1), tokens(2)], 0)
        hat, rstd = both(hat), both(rstd)
        moved = direction - mean(direction) - hat * mean(hat * direction)
        moved = (moved * rstd * gain).astype(bf16)[:, :C]
        dq, dk, dv = (dot(moved, w).astype(bf16) for w in (wq, wk, wv))
        own = [slice(TOK * f, TOK * (f + 1)) for f in range(2)]
        dk_heads = [by_head(dk[o], False) for o in own]
        dv_heads = [by_head(dv[o], False) for o in own]
        mean_d = [mixed(weights, dv_heads[f], dk_heads[f]) for f in range(2)]
        mean_dv = jnp.concatenate([m[0] for m in mean_d], 0)
        mean_dk = jnp.concatenate([m[1] for m in mean_d], 0)
        shifted = with_shift(dq, dq.astype(f32) * both(mean_k) + both(q.astype(f32)) * mean_dk)
        dscores = against(shifted, k_heads, True)
        dscores = dscores + jnp.concatenate([against(q, d, False) for d in dk_heads], 0)
        dweights = (both(probs) * dscores).astype(bf16)
        dblended = (mixed(dweights, v_heads)[0] + mean_dv).astype(bf16)
        image = direction + dot(dblended[:, :C], wo)

        cot = (both(energy) * image).astype(bf16)
        cot = dot_nt(cot[:, :C], out_w_ref[...])
        cot = padded(cot).astype(bf16)
        shifted = with_shift(cot, cot.astype(f32) * both(mean_v))
        cscores = (both(probs) * against(shifted, v_heads, True)).astype(bf16)
        cq = mixed(cscores, k_heads)[0].astype(bf16)
        ck = [transposed_product([q_t], cscores[o])[0] for o in own]
        cv = transposed_product([turned(cot[o]) for o in own], weights)
        turned_part = [dot_tn(ck[f], wk_t) + dot_tn(cv[f], wv_t) for f in range(2)]
        cnormed = padded(dot_nt(cq, wq) + jnp.concatenate(turned_part, 0))
        cnormed = cnormed.astype(bf16).astype(f32) * gain
        back = cnormed - mean(cnormed) - hat * mean(hat * cnormed)
        out = image + back * rstd * both(inverse)
        for f in range(2):
            for l in range(WLEV):
                at = WLEV * t + l
                part = out[TOK * f + PLANE * l : TOK * f + PLANE * (l + 1), :C]
                scaled_ref[f, :, C * at : C * (at + 1)] = part
                back_ref[f, :, C * at : C * (at + 1)] = part[PLANE // 2 :].astype(bf16)
        result = [out[o] for o in own]
        for n, (a, b) in enumerate(((0, 0), (0, 1), (1, 1))):
            totals[n] = totals[n] + jnp.sum(energy * result[a] * result[b], 0, keepdims=True)
    row, found = iota((8, LANE), 0), jnp.zeros((8, LANE), f32)
    for n in range(3):
        found = jnp.where(row == n, jnp.sum(totals[n], -1, keepdims=True), found)
    sums_ref[...] = found


def finish_kernel(total, sums_ref, scaled_ref, back_ref, out_ref):
    sums = sums_ref[...]
    aa, ab, bb = (sums[n : n + 1, :1] for n in range(3))
    first = jnp.sqrt(total / aa)
    second = jnp.sqrt(total / (bb - ab * ab / aa))
    mixing = -ab / aa * second
    edge = back_ref.shape[1]
    for at, ref in ((0, back_ref), (edge, scaled_ref)):
        a = ref[0, :edge, :].astype(jnp.float32)
        b = ref[1, :edge, :].astype(jnp.float32)
        out_ref[at : at + edge, 0, :] = a * first
        out_ref[at : at + edge, 1, :] = b * second + a * mixing


def whole(memory=pltpu.VMEM):
    return pl.BlockSpec(memory_space=memory)


def limit(mib):
    return pltpu.CompilerParams(vmem_limit_bytes=mib * 1024 * 1024)


def prepare(bias_table, bias_index, region, weight):
    packs = TOK + 8 * -(-TOK // 64)
    return pl.pallas_call(
        prepare_kernel,
        out_shape=[
            jax.ShapeDtypeStruct((WTYPES, TOK, KEYS), jnp.float32),
            jax.ShapeDtypeStruct((C, 3 * WIDE), jnp.bfloat16),
        ],
        in_specs=[whole(pltpu.SMEM), whole(), whole(), whole()],
        out_specs=[whole(), whole()],
        scratch_shapes=[pltpu.VMEM((packs, LANE), jnp.int32)] * 2 + [pltpu.VMEM((8, ROWS * LANE), jnp.int32)],
        compiler_params=limit(12),
        cost_estimate=pl.CostEstimate(flops=100000000, bytes_accessed=1400000, transcendentals=0),
        name="prepare",
    )(region.T, bias_index, jnp.transpose(bias_table, (2, 0, 1)), weight)


def window_step(fields, gain, weight, out_weight, bias, energy_table, level_class):
    return pl.pallas_call(
        window_kernel,
        out_shape=[
            jax.ShapeDtypeStruct((2, PLANE, LEV * C), jnp.float32),
            jax.ShapeDtypeStruct((2, PLANE // 2, LEV * C), jnp.bfloat16),
            jax.ShapeDtypeStruct((8, LANE), jnp.float32),
        ],
        in_specs=[whole(pltpu.SMEM)] + [whole()] * 6,
        out_specs=[whole()] * 3,
        compiler_params=limit(24),
        cost_estimate=pl.CostEstimate(flops=2000000000, bytes_accessed=2500000, transcendentals=250000),
        name="window_step",
    )(level_class, fields, gain, weight, out_weight, bias, energy_table)


def finish(total, sums, scaled, back):
    rows = scaled.shape[1]
    return pl.pallas_call(
        functools.partial(finish_kernel, total),
        out_shape=jax.ShapeDtypeStruct((rows, 2, LEV * C), jnp.float32),
        in_specs=[whole()] * 3,
        out_specs=whole(),
        compiler_params=limit(8),
        cost_estimate=pl.CostEstimate(flops=1000000, bytes_accessed=1000000, transcendentals=8),
        name="finish",
    )(sums, scaled, back)


def summed(value, axis):
    size = lax.axis_size(axis)
    if size & (size - 1):
        return lax.psum(value, axis)
    bits = [1 << b for b in range(size.bit_length() - 1)]
    stages = [bits[:1], bits[1:3]] + [[b] for b in bits[3:]]
    for stage in stages:
        offsets = [0]
        for b in stage:
            offsets += [o + b for o in offsets]
        parts = [lax.ppermute(value, axis, [(i, i ^ o) for i in range(size)]) for o in offsets[1:]]
        value = sum(parts, value)
    return value


def local(
    base_state,
    tangents,
    norm_gain,
    qkv_weight,
    out_weight,
    bias_table,
    bias_index,
    region,
    energy_table,
    level_class,
):
    columns = base_state.shape[0]
    size = lax.axis_size("lon")
    up = [(i, (i + 1) % size) for i in range(size)]
    down = [(j, i) for i, j in up]

    def side(start, stop):
        part = jnp.concatenate([base_state[None, start:stop], tangents[:, start:stop]], 0)
        return part.reshape(3, (stop - start) * LAT, LEV * C)

    arrived = lax.ppermute(side(0, HALF), "lon", down)
    bias, weight = prepare(bias_table, bias_index, region, qkv_weight)
    fields = jnp.concatenate([side(HALF, columns), arrived], 1)
    scaled, back, sums = window_step(fields, norm_gain[None], weight, out_weight, bias, energy_table, level_class)
    returned = lax.ppermute(back, "lon", up)
    sums = summed(sums, "lon")
    total = float(columns * size * LAT * LEV * C)
    finished = finish(total, sums, scaled, returned)
    return jnp.transpose(finished.reshape(columns, LAT, 2, LEV * C), (2, 0, 1, 3))


def solution(mesh):
    placed = (
        P(("grp", "lon"), None, None),
        P(None, ("grp", "lon"), None, None),
    ) + (P(),) * 8
    return jax.shard_map(
        local,
        mesh=mesh,
        in_specs=placed,
        out_specs=P(None, ("grp", "lon"), None, None),
        check_vma=False,
    )
```
